32 devices in a mesh: section: 2 (over core), dom: 16 (over z, y, x).
Axes of the slice: x: 2, y: 2, z: 4, core: 2. Of those that a mesh axis runs over, the one named last changes fastest.
Arguments:
- features: bfloat16 [2, 4096, 128], P(None, 'dom'), may hold values from -6 to 6
- cotangent: bfloat16 [2, 4096, 128], P(None, 'dom'), may hold values from -6 to 6
- weights: bfloat16 [2, 2, 128, 256], P('section'), may hold values from -0.5 to 0.5
- edge_tiles: bfloat16 [32, 4, 128, 128], P('dom'), may hold values from -0.375 to 0.375
- source_blocks: int32 [32, 4], P('dom'), may hold values from 0 to 5
- live_counts: int32 [32], P('dom'), may hold values from 1 to 4
Outputs:
- section_outputs: bfloat16 [2, 2, 4096, 128], P('section', None, 'dom')
- boundary_grads: bfloat16 [2, 2, 4096, 128], P('section', None, 'dom')
- weight_grads: float32 [2, 2, 128, 256], P('section')
The draws below stay inside these ranges and needn't reach their ends.
Inputs may be any that keep to these rules, and one draw needn't show every extreme that they name: `source_blocks`: index into the partition's extended list: its 2 blocks before, its 2 own blocks, its 2 blocks after.
All inputs are finite; a program needn't handle non-finite values.
Results may differ from the reference program's by a relative error of at most 0.017.
Values may be sent and summed in bfloat16 or wider, within the bound.
No kernel may reach another device: no remote copies, remote signals or barrier semaphores. Data moves between devices by JAX's collectives and lax.ppermute only.
A program may use at most 64 MiB of HBM per device.

```python
import math
import jax
import jax.numpy as jnp
from jax import lax

H = 128
TILE = 128
KMAX = 4
HB = 2
NB = 2
LPS = 2
MB = 2
NBLK = 32
NODES = 4096
N_SECTION = 2
N_DOM = 16


def place_ends(result, key, smallest, top_value):
    extent = result.shape
    index_at = [jax.random.randint(jax.random.fold_in(key, axis), (), 0, extent[axis]) for axis in range(len(extent))]
    result = result.at[tuple(index_at)].set(smallest)
    longest = extent.index(max(extent))
    index_at[longest] = (index_at[longest] + 1) % extent[longest]
    return result.at[tuple(index_at)].set(top_value)


def level_of(key, shape, cuts, low, largest):
    factor_of, own = 1.0, jax.random.fold_in(key, 6)
    for dim, parts in cuts:
        draws = jnp.exp(jax.random.uniform(jax.random.fold_in(own, dim), (parts,), jnp.float32, low / len(cuts), largest / len(cuts)))
        factor_of = factor_of * jnp.repeat(draws, shape[dim] // parts).reshape([-1 if axis == dim else 1 for axis in range(len(shape))])
    return factor_of


def gaussian(rng, dims, scale, most, shards=(), kind=jnp.bfloat16):
    factor_of = level_of(rng, dims, shards, -0.22, 0.18) if shards else 1.0
    array = jax.random.normal(rng, dims, jnp.float32) * scale * factor_of
    return jnp.minimum(jnp.maximum(array, -most), most).astype(kind)


def setup_inputs(seed: int = 0) -> dict:
    arg_keys = jax.random.split(jax.random.key(seed), 7)
    features = gaussian(arg_keys[0], (MB, NODES, H), 1.0, 6.0, ((1, 16),))
    cotangent = gaussian(arg_keys[1], (MB, NODES, H), 1.0, 6.0, ((1, 16),))
    weights = gaussian(arg_keys[2], (N_SECTION, LPS, H, 2 * H), H ** -0.5, 0.5, ((0, 2),))
    edge_tiles = gaussian(arg_keys[3], (NBLK, KMAX, TILE, TILE), (2 * TILE) ** -0.5, 0.375, ((0, 16),))
    source_blocks = place_ends(jax.random.randint(arg_keys[4], (NBLK, KMAX), 0, NB + 2 * HB), jax.random.fold_in(arg_keys[4], 1), 0, (NB + 2 * HB) - 1).astype(jnp.int32)
    live_counts = place_ends(jax.random.randint(arg_keys[5], (NBLK,), 1, KMAX + 1), jax.random.fold_in(arg_keys[5], 1), 1, KMAX).astype(jnp.int32)
    return dict(features=features, cotangent=cotangent, weights=weights, edge_tiles=edge_tiles, source_blocks=source_blocks, live_counts=live_counts)


def layer_forward(hidden, weight, masked, source_parts):
    projected = jnp.dot(hidden, weight, preferred_element_type=jnp.float32)
    message_rows = projected[:, :H].astype(jnp.bfloat16).reshape(NBLK, TILE, H)
    rim_zero = jnp.zeros((HB, TILE, H), jnp.bfloat16)
    padded = jnp.concatenate([rim_zero, message_rows, rim_zero], 0)

    def per_part(part_idx):
        extended = lax.dynamic_slice_in_dim(padded, part_idx * NB, NB + 2 * HB, 0)
        gathered = extended[source_parts[part_idx]].astype(jnp.float32)
        return jnp.einsum('bkij,bkjh->bih', masked[part_idx].astype(jnp.float32), gathered, precision=lax.Precision.HIGHEST)
    aggregate = lax.map(per_part, jnp.arange(N_DOM, dtype=jnp.int32))
    pre_act = aggregate.reshape(NODES, H) + projected[:, H:]
    squashed = jnp.tanh(pre_act)
    return ((hidden.astype(jnp.float32) + squashed).astype(jnp.bfloat16), squashed)

def layer_backward(hidden, squashed, gradient, weight, masked, onehot):
    pre_grad = gradient * (1.0 - squashed * squashed)
    pre_low = pre_grad.astype(jnp.bfloat16)
    pre_blocks = pre_low.reshape(N_DOM, NB, TILE, H)

    def per_part(part_idx):
        spread = jnp.einsum('bkij,bih->bkjh', masked[part_idx].astype(jnp.float32), pre_blocks[part_idx].astype(jnp.float32), precision=lax.Precision.HIGHEST)
        return jnp.einsum('bke,bkjh->ejh', onehot[part_idx], spread, precision=lax.Precision.HIGHEST)
    ext_grad = lax.map(per_part, jnp.arange(N_DOM, dtype=jnp.int32))
    own_rows = ext_grad[:, HB:HB + NB]
    from_before = jnp.concatenate([jnp.zeros((1, HB, TILE, H), jnp.float32), ext_grad[:-1, HB + NB:]], 0)
    from_after = jnp.concatenate([ext_grad[1:, :HB], jnp.zeros((1, HB, TILE, H), jnp.float32)], 0)
    own_rows = own_rows.at[:, :HB].add(from_before)
    own_rows = own_rows.at[:, NB - HB:].add(from_after)
    source_low = own_rows.reshape(NODES, H).astype(jnp.bfloat16)
    paired = jnp.concatenate([source_low, pre_low], 1)
    layer_grad = jnp.dot(hidden.T, paired, preferred_element_type=jnp.float32)
    gradient = gradient + jnp.dot(paired, weight.T, preferred_element_type=jnp.float32)
    return (gradient, layer_grad)

def reference(features, cotangent, weights, edge_tiles, source_blocks, live_counts):
    live = jnp.arange(KMAX, dtype=jnp.int32)[None, :] < live_counts[:, None]
    masked = jnp.where(live[:, :, None, None], edge_tiles, jnp.zeros((), jnp.bfloat16))
    masked = masked.reshape(N_DOM, NB, KMAX, TILE, TILE)
    source_parts = source_blocks.reshape(N_DOM, NB, KMAX)
    onehot = (source_parts[..., None] == jnp.arange(NB + 2 * HB, dtype=jnp.int32)).astype(jnp.float32)
    section_rows = [[] for section_idx in range(N_SECTION)]
    bound_rows = [[None] * MB for section_idx in range(N_SECTION)]
    grad_total = jnp.zeros((N_SECTION, LPS, H, 2 * H), jnp.float32)
    for batch_idx in range(MB):
        hidden = features[batch_idx]
        stash_inputs = {}
        for section_idx in range(N_SECTION):
            for layer_idx in range(LPS):
                before = hidden
                hidden, squashed = layer_forward(hidden, weights[section_idx, layer_idx], masked, source_parts)
                stash_inputs[section_idx, layer_idx] = (before, squashed)
            section_rows[section_idx].append(hidden)
        gradient = cotangent[batch_idx].astype(jnp.float32)
        for section_idx in reversed(range(N_SECTION)):
            for layer_idx in reversed(range(LPS)):
                before, squashed = stash_inputs[section_idx, layer_idx]
                gradient, layer_grad = layer_backward(before, squashed, gradient, weights[section_idx, layer_idx], masked, onehot)
                grad_total = grad_total.at[section_idx, layer_idx].add(layer_grad)
            rounded = gradient.astype(jnp.bfloat16)
            bound_rows[section_idx][batch_idx] = rounded
            gradient = rounded.astype(jnp.float32)
    section_outputs = jnp.stack([jnp.stack(section_rows[section_idx]) for section_idx in range(N_SECTION)])
    boundary_grads = jnp.stack([jnp.stack(bound_rows[section_idx]) for section_idx in range(N_SECTION)])
    weight_grads = grad_total * (1.0 / math.sqrt(MB * NODES))
    return (section_outputs, boundary_grads, weight_grads)
```

```python
import functools
import math

import jax
import jax.numpy as jnp
from jax import lax
from jax.experimental import pallas as pl
from jax.experimental.pallas import tpu as pltpu
from jax.sharding import PartitionSpec as P

HB = 2
BOTH = ("section", "dom")
NT = (((1,), (1,)), ((), ()))
TN = (((0,), (0,)), ((), ()))


def pair_chain(mesh):
    count = mesh.shape["dom"]
    pairs = count // 2
    order = list(range(pairs))
    chips = mesh.devices.reshape(-1, count)[0]
    coords = [getattr(chips[2 * u], "coords", None) for u in order]
    if coords[0] is None:
        return order
    run = 1
    while run < pairs and sum(a != b for a, b in zip(coords[run], coords[0])) == 1 and pairs % run == 0:
        same = [i for i in range(3) if coords[1][i] != coords[0][i]]
        if any(coords[run][i] != coords[0][i] for i in range(3) if i not in same):
            break
        run += 1
    chain = []
    for start in range(0, pairs, run):
        part = order[start : start + run]
        chain += part[::-1] if (start // run) % 2 else part
    return chain


def routes(mesh):
    count = mesh.shape["dom"]
    chain = pair_chain(mesh)
    worker = {(m, p): (p % 2) * count + 2 * chain[p // 2] + m for m in range(2) for p in range(count)}
    home = lambda s, p: s * count + p
    spread = [(home(1 - m, p), worker[m, p]) for m in range(2) for p in range(count)]
    other = [(worker[m, p], home(1 - m, p)) for m in range(2) for p in range(count)]
    same = [(worker[m, p], home(m, p)) for m in range(2) for p in range(count)]
    fixed = [a for a, b in same if a == b]
    same = [(a, b) for a, b in same if a != b]
    same += [(a, fixed[i ^ 1]) for i, a in enumerate(fixed)]
    across = []
    for m in range(2):
        for p in range(1, count - 1, 2):
            across += [(worker[m, p], worker[m, p + 1]), (worker[m, p + 1], worker[m, p])]
    for p in (0, count - 1):
        across += [(worker[0, p], worker[1, p]), (worker[1, p], worker[0, p])]
    keeps = [i in fixed for i in range(2 * count)]
    return spread, same, other, across, keeps


def kernel_call(body, outs, scratch, smem, flops):
    def call(*args):
        specs = [pl.BlockSpec(memory_space=pltpu.SMEM if i < smem else pltpu.VMEM) for i in range(len(args))]
        moved = sum(math.prod(o.shape) * o.dtype.itemsize for o in outs)
        moved += sum(math.prod(a.shape) * a.dtype.itemsize for a in args)
        return pl.pallas_call(
            body,
            out_shape=outs,
            in_specs=specs,
            out_specs=[pl.BlockSpec(memory_space=pltpu.VMEM)] * len(outs),
            scratch_shapes=scratch,
            compiler_params=pltpu.CompilerParams(vmem_limit_bytes=12 << 20),
            cost_estimate=pl.CostEstimate(flops=flops, bytes_accessed=moved, transcendentals=0),
        )(*args)

    return call


def forward_step(slots, h_ref, on_ref, off_ref, w_ref, a_ref, ext, gath):
    rows, width = h_ref.shape
    blocks, tile, span = a_ref.shape
    count = span // tile
    ext[0:HB] = on_ref[...].reshape(HB, tile, width)
    ext[HB : HB + blocks] = h_ref[...].reshape(blocks, tile, width)
    ext[HB + blocks :] = off_ref[...].reshape(HB, tile, width)
    parts = []
    for b in range(blocks):
        for k in range(count):
            gath[b, k * tile : (k + 1) * tile, :] = ext[slots[b * count + k]]
        parts.append(jnp.dot(a_ref[b], gath[b], preferred_element_type=jnp.float32))
    mixed = jnp.concatenate(parts, 0).astype(jnp.bfloat16)
    hidden = h_ref[...]
    pre = jnp.dot(mixed, w_ref[:, :width], preferred_element_type=jnp.float32)
    pre += jnp.dot(hidden, w_ref[:, width:], preferred_element_type=jnp.float32)
    squashed = jnp.tanh(pre)
    return (hidden.astype(jnp.float32) + squashed).astype(jnp.bfloat16), mixed, squashed


def backward_step(slots, gradient, squashed, at_ref, low_ref, own_ref, on_ref, off_ref, ext):
    blocks, span, tile = at_ref.shape
    count = span // tile
    rows, width = gradient.shape
    low = (gradient * (1.0 - squashed * squashed)).astype(jnp.bfloat16)
    low_ref[...] = low
    ext[...] = jnp.zeros_like(ext)
    for b in range(blocks):
        sent = jnp.dot(at_ref[b], low[b * tile : (b + 1) * tile], preferred_element_type=jnp.float32)
        for k in range(count):
            slot = slots[b * count + k]
            ext[slot] = ext[slot] + sent[k * tile : (k + 1) * tile]
    on_ref[...] = ext[0:HB].reshape(HB * tile, width).astype(jnp.bfloat16)
    own_ref[...] = ext[HB : HB + blocks].reshape(rows, width)
    off_ref[...] = ext[HB + blocks :].reshape(HB * tile, width).astype(jnp.bfloat16)


def finish_step(grad_ref, low_ref, own_ref, on_ref, off_ref, w_ref):
    total = own_ref[...] + on_ref[...].astype(jnp.float32) + off_ref[...].astype(jnp.float32)
    paired = jnp.concatenate([total.astype(jnp.bfloat16), low_ref[...]], 1)
    return grad_ref[...].astype(jnp.float32) + lax.dot_general(
        paired, w_ref[...], NT, preferred_element_type=jnp.float32
    )


def forward_kernel(slots, h, on, off, w, a, out, mixed, squashed, ext, gath):
    out[...], mixed[...], squashed[...] = forward_step(slots, h, on, off, w, a, ext, gath)


def turn_kernel(slots, h, on, off, w, a, at, cot, out, mixed, low, own, s_on, s_off, ext, gath, acc):
    out[...], mixed[...], squashed = forward_step(slots, h, on, off, w, a, ext, gath)
    backward_step(slots, cot[...].astype(jnp.float32), squashed, at, low, own, s_on, s_off, acc)


def backward_kernel(edge, slots, grad, low, own, on, off, w, squashed, at, *rest):
    if edge:
        bound, low_out, own_out, s_on, s_off, acc = rest
        bound[...] = finish_step(grad, low, own, on, off, w).astype(jnp.bfloat16)
        gradient = bound[...].astype(jnp.float32)
    else:
        full, low_out, own_out, s_on, s_off, acc = rest
        gradient = finish_step(grad, low, own, on, off, w)
        full[...] = gradient
    backward_step(slots, gradient, squashed[...], at, low_out, own_out, s_on, s_off, acc)


def finish_kernel(grad, low, own, on, off, w, bound):
    bound[...] = finish_step(grad, low, own, on, off, w).astype(jnp.bfloat16)


def reduce_dom(total):
    count = lax.axis_size("dom")
    stride = 1
    while count // stride % 2 == 0:
        total = lax.reduce_precision(total, 8, 7)
        got = lax.ppermute(total.astype(jnp.bfloat16), "dom", [(i, i ^ stride) for i in range(count)])
        total = total + got.astype(jnp.float32)
        stride *= 2
    left = count // stride
    if left > 1:
        low = total.astype(jnp.bfloat16)
        place = lax.axis_index("dom") // stride
        terms = [low]
        for hop in range(1, left):
            terms.append(lax.ppermute(low, "dom", [((i + hop * stride) % count, i) for i in range(count)]))
        stack = jnp.stack(terms + terms).astype(jnp.float32)
        total = jnp.sum(lax.dynamic_slice_in_dim(stack, (left - place) % left, left, 0), 0)
    return total


def local(plan, features, cotangent, weights, edge_tiles, source_blocks, live_counts):
    spread, same, other, across, keeps = plan
    core = lax.axis_index("section")
    chip = lax.axis_index("dom")
    chips = lax.axis_size("dom")
    micro_count, rows, width = features.shape
    layers = weights.shape[1]
    blocks, slot_count, tile = edge_tiles.shape[:3]
    if blocks != HB or micro_count != 2 or lax.axis_size("section") != 2:
        raise ValueError("unsupported sizes")
    scale = 1.0 / math.sqrt(micro_count * rows * chips)
    swap = lambda x: lax.ppermute(x, "section", [(0, 1), (1, 0)])
    cross = lambda x: lax.ppermute(x, BOTH, across)
    place = lambda x: lax.ppermute(x, BOTH, spread)

    def exchange(to_on, to_off):
        off = cross(to_off)
        return swap(to_on), off


    hidden = place(lax.dynamic_index_in_dim(features, 1 - core, 0, keepdims=False))
    partner = swap(weights[0])
    first = jnp.where(core == 0, weights[0], partner)
    second = jnp.where(core == 0, partner, weights[0])
    layer_weights = [first[i] for i in range(layers)] + [second[i] for i in range(layers)]

    live = lax.broadcasted_iota(jnp.int32, (blocks, slot_count), 1) < live_counts[:, None]
    live &= ~((source_blocks < HB) & (chip == 0))
    live &= ~((source_blocks >= HB + blocks) & (chip == chips - 1))
    even = chip % 2 == 0
    shifted = jnp.where(source_blocks < HB, source_blocks + HB + blocks, source_blocks)
    shifted = jnp.where(source_blocks >= HB + blocks, source_blocks - HB - blocks, shifted)
    slots = place(jnp.where(even, shifted, source_blocks).reshape(-1))
    masked = place(jnp.where(live[:, :, None, None], edge_tiles, jnp.zeros((), jnp.bfloat16)))
    gradient = place(lax.dynamic_index_in_dim(cotangent, 1 - core, 0, keepdims=False))
    ahead = masked.transpose(0, 2, 1, 3).reshape(blocks, tile, slot_count * tile)
    behind = masked.transpose(0, 1, 3, 2).reshape(blocks, slot_count * tile, tile)

    low_shape = jax.ShapeDtypeStruct((rows, width), jnp.bfloat16)
    full_shape = jax.ShapeDtypeStruct((rows, width), jnp.float32)
    ext_blocks = blocks + 2 * HB
    ext = pltpu.VMEM((ext_blocks, tile, width), jnp.bfloat16)
    gath = pltpu.VMEM((blocks, slot_count * tile, width), jnp.bfloat16)
    acc = pltpu.VMEM((ext_blocks, tile, width), jnp.float32)
    flops = 2 * rows * width * (slot_count * tile + 2 * width)

    forward = kernel_call(forward_kernel, [low_shape, low_shape, full_shape], [ext, gath], 1, flops)
    turn = kernel_call(
        turn_kernel, [low_shape] * 3 + [full_shape, low_shape, low_shape], [ext, gath, acc], 1, 2 * flops
    )
    sends = [low_shape, full_shape, low_shape, low_shape]
    inner = kernel_call(functools.partial(backward_kernel, False), [full_shape] + sends, [acc], 1, flops)
    edge = kernel_call(functools.partial(backward_kernel, True), [low_shape] + sends, [acc], 1, flops)
    finish = kernel_call(finish_kernel, [low_shape], [], 0, flops)

    total_layers = 2 * layers
    saved = []
    outputs = []
    for idx in range(total_layers - 1):
        before = hidden
        hidden, mixed, squashed = forward(
            slots, before, *exchange(before, before), layer_weights[idx], ahead
        )
        saved.append((before, mixed, squashed))
        if idx + 1 == layers:
            outputs.append(hidden)
    before = hidden
    hidden, mixed, low, own, to_on, to_off = turn(
        slots, before, *exchange(before, before), layer_weights[-1], ahead, behind, gradient
    )
    outputs.append(hidden)

    def weight_term(before, mixed, low):
        return jnp.concatenate(
            [
                lax.dot_general(mixed, low, TN, preferred_element_type=jnp.float32),
                lax.dot_general(before, low, TN, preferred_element_type=jnp.float32),
            ],
            1,
        )

    terms = [None] * total_layers
    terms[-1] = weight_term(before, mixed, low)
    bounds = [None, None]
    for idx in reversed(range(total_layers - 1)):
        before, mixed, squashed = saved[idx]
        step = edge if idx + 1 == layers else inner
        gradient, low, own, to_on, to_off = step(
            slots, gradient, low, own, *exchange(to_on, to_off), layer_weights[idx + 1], squashed, behind
        )
        if idx + 1 == layers:
            bounds[1] = gradient
        terms[idx] = weight_term(before, mixed, low)
    bounds[0] = finish(gradient, low, own, *exchange(to_on, to_off), layer_weights[0])[0]

    micro = chip % 2 == 0
    stays = jnp.asarray(keeps)[core * chips + chip]

    def home(pair):
        kept = jnp.where(micro, pair[0], pair[1])
        got_same = jnp.where(stays, kept, lax.ppermute(kept, BOTH, same))
        got_other = lax.ppermute(jnp.where(micro, pair[1], pair[0]), BOTH, other)
        return jnp.where(
            core == 0, jnp.stack([got_same, got_other]), jnp.stack([got_other, got_same])
        )[None]

    section_rows = home(outputs)
    bound_rows = home(bounds)
    low_half = jnp.stack(terms[:layers])
    high_half = jnp.stack(terms[layers:])
    got = swap(jnp.where(core == 0, high_half, low_half).astype(jnp.bfloat16))
    total = jnp.where(core == 0, low_half, high_half) + got.astype(jnp.float32)
    weight_grads = reduce_dom(total) * scale
    return section_rows, bound_rows, weight_grads[None]


def solution(mesh):
    placed = (
        P(None, "dom", None),
        P(None, "dom", None),
        P("section", None, None, None),
        P("dom", None, None, None),
        P("dom", None),
        P("dom"),
    )
    return jax.shard_map(
        functools.partial(local, routes(mesh)),
        mesh=mesh,
        in_specs=placed,
        out_specs=(
            P("section", None, "dom", None),
            P("section", None, "dom", None),
            P("section", None, None, None),
        ),
        check_vma=False,
    )
```
